32 devices in a mesh: tm: 16 (over z, y, core), head: 2 (over x).
Axes of the slice: x: 2, y: 2, z: 4, core: 2. Of those that a mesh axis runs over, the one named last changes fastest.
Arguments:
- frames: bfloat16 [32768, 1024], P('tm'), may hold values from -28 to 28
- w_query: bfloat16 [1024, 1024], P(None, 'head'), may hold values from -0.5 to 0.5
- w_key: bfloat16 [1024, 1024], P(None, 'head'), may hold values from -0.7 to 0.7
- w_value: bfloat16 [1024, 1024], P(None, 'head'), may hold values from -0.1875 to 0.1875
- w_out: bfloat16 [1024, 1024], replicated, may hold values from -0.5 to 0.5
Outputs:
- mixed: bfloat16 [32768, 1024], P('tm', 'head')
The draws below stay inside these ranges and needn't reach their ends.
All inputs are finite; a program needn't handle non-finite values.
Results may differ from the reference program's by a relative error of at most 0.013.
Values may be sent and summed in bfloat16 or wider, within the bound.
A program may use at most 128 MiB of HBM per device.

```python
import jax
import jax.numpy as jnp
from jax import lax

D = 1024
HEADS = 16
DH = 64
BLK = 2048
WIN = 512
PK = 256
LEVELS = 4
FRAMES = 32768


def shared_rows(key):
    return jnp.clip(jax.random.normal(jax.random.fold_in(key, 11), (D, D), jnp.float32), -4.0, 4.0)


def draw_w_query(key, part):
    return (shared_rows(key) * D ** (-0.5)).astype(jnp.bfloat16)


def draw_w_key(key, part):
    noise = jnp.clip(jax.random.normal(jax.random.fold_in(key, 12), (D, D), jnp.float32), -4.0, 4.0)
    return ((0.6 * shared_rows(key) + 0.8 * noise) * D ** (-0.5)).astype(jnp.bfloat16)


def draw_frames(key, part):
    slot_len = BLK // PK
    slots = FRAMES // slot_len
    blocks = FRAMES // BLK
    block_scale = jnp.exp(jax.random.uniform(jax.random.fold_in(key, 31), (blocks,), jnp.float32, -1.0, 1.0))
    frame_scale = jnp.repeat(block_scale, BLK, axis=0)
    base = jnp.clip(jax.random.normal(jax.random.fold_in(key, 26), (slots, D), jnp.float32), -4.0, 4.0)
    jitter = jnp.clip(jax.random.normal(jax.random.fold_in(key, 27), (FRAMES, D), jnp.float32), -4.0, 4.0)
    result = jnp.clip((jnp.repeat(base, slot_len, axis=0) + 0.5 * jitter) * frame_scale[:, None], -6.0, 6.0)
    return result.astype(jnp.bfloat16)


def steps_of(key, dims, pieces, low, largest):
    factor_of, own = 1.0, jax.random.fold_in(key, 6)
    for dim, blocks in pieces:
        heights = jnp.exp(jax.random.uniform(jax.random.fold_in(own, dim), (blocks,), jnp.float32, low / len(pieces), largest / len(pieces)))
        factor_of = factor_of * jnp.repeat(heights, dims[dim] // blocks).reshape([-1 if axis == dim else 1 for axis in range(len(dims))])
    return factor_of


def gaussian(own_key, extent, spread, most, shards=(), held_as=jnp.bfloat16):
    gain = steps_of(own_key, extent, shards, -0.22, 0.18) if shards else 1.0
    values = jax.random.normal(own_key, extent, jnp.float32) * spread * gain
    return jnp.minimum(jnp.maximum(values, -most), most).astype(held_as)


def setup_inputs(seed: int = 0) -> dict:
    seeds = jax.random.split(jax.random.key(seed), 6)
    frames = draw_frames(jax.random.fold_in(seeds[5], 71), 0)
    w_query = draw_w_query(jax.random.fold_in(seeds[5], 71), 0)
    w_key = draw_w_key(jax.random.fold_in(seeds[5], 71), 0)
    w_value = gaussian(seeds[3], (D, D), D ** -0.5, 0.1875, ((1, 2),))
    w_out = gaussian(seeds[4], (D, D), (D // 8) ** -0.5, 0.5)
    return dict(frames=frames, w_query=w_query, w_key=w_key, w_value=w_value, w_out=w_out)


def reference(frames, w_query, w_key, w_value, w_out):
    queries = jnp.dot(frames, w_query, preferred_element_type=jnp.float32).astype(jnp.bfloat16)
    keys = jnp.dot(frames, w_key, preferred_element_type=jnp.float32).astype(jnp.bfloat16)
    values = jnp.dot(frames, w_value, preferred_element_type=jnp.float32).astype(jnp.bfloat16)
    blocks = FRAMES // BLK
    pooled_keys = keys.astype(jnp.float32).reshape(blocks, PK, BLK // PK, D).mean(axis=2).astype(jnp.bfloat16)
    pooled_values = values.astype(jnp.float32).reshape(blocks, PK, BLK // PK, D).mean(axis=2).astype(jnp.bfloat16)
    qrows = min(512, BLK)
    scale = DH ** -0.5

    def one_block(index):
        start = index * BLK
        own_q = lax.dynamic_slice_in_dim(queries, start, BLK, 0)
        own_k = lax.dynamic_slice_in_dim(keys, start, BLK, 0)
        own_v = lax.dynamic_slice_in_dim(values, start, BLK, 0)
        rim_start = jnp.maximum(start - WIN, 0).astype(jnp.int32)
        rim_k = lax.dynamic_slice_in_dim(keys, rim_start, WIN, 0)
        rim_v = lax.dynamic_slice_in_dim(values, rim_start, WIN, 0)
        key_list = [own_k, rim_k]
        value_list = [own_v, rim_v]
        valid_list = [jnp.full((WIN,), index >= 1)]
        for level in range(LEVELS):
            dist = 2 ** level
            source = jnp.maximum(index - dist, 0).astype(jnp.int32)
            key_list.append(lax.dynamic_index_in_dim(pooled_keys, source, 0, keepdims=False))
            value_list.append(lax.dynamic_index_in_dim(pooled_values, source, 0, keepdims=False))
            valid_list.append(jnp.full((PK,), index >= dist))
        all_k = jnp.concatenate(key_list, 0).astype(jnp.float32).reshape(-1, HEADS, DH)
        all_v = jnp.concatenate(value_list, 0).astype(jnp.float32).reshape(-1, HEADS, DH)
        extra_valid = jnp.concatenate(valid_list, 0)
        total = all_k.shape[0]
        outputs = []
        for sub in range(BLK // qrows):
            query_part = own_q[sub * qrows:(sub + 1) * qrows].astype(jnp.float32).reshape(qrows, HEADS, DH)
            score = jnp.einsum("qhd,khd->hqk", query_part, all_k) * scale
            qpos = sub * qrows + jnp.arange(qrows, dtype=jnp.int32)
            kpos = jnp.arange(total, dtype=jnp.int32)
            causal = kpos[None, :] <= qpos[:, None]
            outside = jnp.concatenate([jnp.zeros((BLK,), dtype=bool), extra_valid], 0)
            allowed = jnp.where(kpos[None, :] < BLK, causal, outside[None, :])
            score = jnp.where(allowed[None], score, jnp.float32(-1e30))
            top = jnp.max(score, axis=-1, keepdims=True)
            expo = jnp.where(allowed[None], jnp.exp(score - top), jnp.float32(0.0))
            weight = (expo / jnp.sum(expo, axis=-1, keepdims=True)).astype(jnp.bfloat16)
            context = jnp.einsum("hqk,khd->qhd", weight.astype(jnp.float32), all_v)
            outputs.append(context.reshape(qrows, D).astype(jnp.bfloat16))
        return jnp.concatenate(outputs, 0)

    context = lax.map(one_block, jnp.arange(blocks, dtype=jnp.int32)).reshape(FRAMES, D)
    return jnp.dot(context, w_out, preferred_element_type=jnp.float32).astype(jnp.bfloat16)
```

```python
import functools
import math

import jax
import jax.numpy as jnp
from jax import lax
from jax.experimental import pallas as pl
from jax.experimental.pallas import tpu as pltpu
from jax.sharding import PartitionSpec as P

DH = 64
WIN = 512
PK = 256
SUMS = 16
STATE = DH + SUMS + 8
BQ = 512
BK = 512
NEG = -1e30


def step(k, q, v, state, mask=None):
    top, acc = state
    s = jnp.dot(k, q, preferred_element_type=jnp.float32)
    if mask is not None:
        s = jnp.where(mask, s, NEG)
    here = jnp.max(s, axis=0, keepdims=True)
    if top is None:
        p = jnp.exp2(s - here).astype(jnp.bfloat16)
        return here, jnp.dot(v, p, preferred_element_type=jnp.float32)
    new = jnp.maximum(top, here)
    p = jnp.exp2(s - new).astype(jnp.bfloat16)
    acc = acc * jnp.exp2(top - new) + jnp.dot(v, p, preferred_element_type=jnp.float32)
    return new, acc


def head_queries(q):
    first = lax.broadcasted_iota(jnp.int32, q.shape, 0) < DH
    zero = jnp.zeros_like(q)
    return jnp.where(first, q, zero), jnp.where(first, zero, q)


def local_kernel(q_ref, k_ref, v_ref, out_ref):
    index = pl.program_id(1)
    bq = q_ref.shape[1]
    qs = head_queries(q_ref[...])
    ones = jnp.ones((SUMS, bq), jnp.bfloat16)

    def tile(j, states, mask):
        rows = pl.ds(pl.multiple_of(j * bq, bq), bq)
        k = k_ref[rows, :]
        result = []
        for h in range(2):
            v = jnp.concatenate([v_ref[h * DH : (h + 1) * DH, rows], ones], 0)
            result.append(step(k, qs[h], v, states[h], mask))
        return tuple(result)

    mask = lax.broadcasted_iota(jnp.int32, (bq, bq), 0) <= lax.broadcasted_iota(
        jnp.int32, (bq, bq), 1
    )
    states = tile(index, ((None, None), (None, None)), mask)
    states = lax.fori_loop(0, index, lambda j, st: tile(j, st, None), states)
    for h in range(2):
        top, acc = states[h]
        out_ref[h, : DH + SUMS] = acc
        out_ref[h, DH + SUMS :] = jnp.broadcast_to(top, (8, bq))


def remote_kernel(q_ref, state_ref, k_ref, v_ref, ones_ref, out_ref):
    qs = head_queries(q_ref[...])
    total = k_ref.shape[0]
    states = [
        (state_ref[h, DH + SUMS : DH + SUMS + 1], state_ref[h, : DH + SUMS]) for h in range(2)
    ]
    for start in range(0, total, BK):
        stop = min(total, start + BK)
        k = k_ref[start:stop]
        for h in range(2):
            v = jnp.concatenate(
                [v_ref[h * DH : (h + 1) * DH, start:stop], ones_ref[:, start:stop]], 0
            )
            states[h] = step(k, qs[h], v, states[h])
    for h in range(2):
        acc = states[h][1]
        out_ref[h * DH : (h + 1) * DH] = (acc[:DH] / acc[DH : DH + 1]).astype(jnp.bfloat16)


def local_attention(q_t, keys, v_t):
    width, block = q_t.shape
    pairs = width // (2 * DH)
    bq = min(BQ, block)
    return pl.pallas_call(
        local_kernel,
        grid=(pairs, block // bq),
        in_specs=[
            pl.BlockSpec((2 * DH, bq), lambda p, i: (p, i)),
            pl.BlockSpec((block, 2 * DH), lambda p, i: (0, p)),
            pl.BlockSpec((2 * DH, block), lambda p, i: (p, 0)),
        ],
        out_specs=pl.BlockSpec((2, STATE, bq), lambda p, i: (p, 0, i)),
        out_shape=jax.ShapeDtypeStruct((2 * pairs, STATE, block), jnp.float32),
        compiler_params=pltpu.CompilerParams(vmem_limit_bytes=48 * 2**20),
        cost_estimate=pl.CostEstimate(
            flops=8 * width * block * block, bytes_accessed=8 * width * block, transcendentals=0
        ),
    )(q_t, keys, v_t)


def remote_attention(chunk, q_t, state, keys, v_t, ones):
    width, block = q_t.shape
    pairs = width // (2 * DH)
    bq = min(BQ, block)
    total = keys.shape[0]
    return pl.pallas_call(
        remote_kernel,
        grid=(pairs,),
        in_specs=[
            pl.BlockSpec((2 * DH, bq), lambda p: (p, chunk)),
            pl.BlockSpec((2, STATE, bq), lambda p: (p, 0, chunk)),
            pl.BlockSpec((total, 2 * DH), lambda p: (0, p)),
            pl.BlockSpec((2 * DH, total), lambda p: (p, 0)),
            pl.BlockSpec((SUMS, total), lambda p: (0, 0)),
        ],
        out_specs=pl.BlockSpec((2 * DH, bq), lambda p: (p, 0)),
        out_shape=jax.ShapeDtypeStruct((width, bq), jnp.bfloat16),
        compiler_params=pltpu.CompilerParams(vmem_limit_bytes=48 * 2**20),
        cost_estimate=pl.CostEstimate(
            flops=16 * width * bq * total, bytes_accessed=8 * width * total, transcendentals=0
        ),
    )(q_t, state, keys, v_t, ones)


def from_behind(value, steps):
    count = lax.axis_size("tm")
    return lax.ppermute(value, "tm", [(s, s + steps) for s in range(count - steps)])


def body(frames, w_query, w_key, w_value, w_out):
    block = frames.shape[0]
    width = w_query.shape[1]
    blocks = lax.axis_size("tm")
    sides = lax.axis_size("head")
    depth = 0
    while 2**depth < blocks:
        depth = depth + 1
    here = lax.axis_index("tm")
    side = lax.axis_index("head")
    across = (((0,), (1,)), ((), ()))
    keys = jnp.dot(frames, w_key, preferred_element_type=jnp.float32).astype(jnp.bfloat16)
    v_t = lax.dot_general(w_value, frames, across, preferred_element_type=jnp.float32).astype(
        jnp.bfloat16
    )
    factor = DH**-0.5 * math.log2(math.e)
    q_t = (
        lax.dot_general(w_query, frames, across, preferred_element_type=jnp.float32) * factor
    ).astype(jnp.bfloat16)
    span = block // PK
    pool = jnp.where(
        jnp.arange(block)[:, None] // span == jnp.arange(PK)[None, :], 1.0 / span, 0.0
    ).astype(jnp.bfloat16)
    pooled_k = lax.dot_general(
        pool, keys, (((0,), (0,)), ((), ())), preferred_element_type=jnp.float32
    ).astype(jnp.bfloat16)
    pooled_v = jnp.dot(v_t, pool, preferred_element_type=jnp.float32).astype(jnp.bfloat16)

    got_k = [from_behind(keys[block - WIN :], 1)]
    got_v = [from_behind(v_t[:, block - WIN :], 1)]
    valid = [jnp.full((WIN,), here >= 1)]
    for level in range(depth):
        got_k.append(from_behind(pooled_k, 2**level))
        got_v.append(from_behind(pooled_v, 2**level))
        valid.append(jnp.full((PK,), here >= 2**level))
    valid = jnp.concatenate(valid, 0)
    state = local_attention(q_t, keys, v_t)
    far_k = jnp.where(valid[:, None], jnp.concatenate(got_k, 0), keys[:1])
    far_v = jnp.concatenate(got_v, 1)
    ones = jnp.broadcast_to(valid[None, :], (SUMS, valid.shape[0])).astype(jnp.bfloat16)

    mine = lax.dynamic_slice_in_dim(w_out, side * width, width, 1)
    w_rows = [
        lax.dynamic_slice_in_dim(mine, ((side + s) % sides) * width, width, 0)
        for s in range(sides)
    ]
    bq = min(BQ, block)
    outputs = []
    for chunk in range(block // bq):
        part = remote_attention(chunk, q_t, state, far_k, far_v, ones)
        total = lax.dot_general(
            part, w_rows[0], (((0,), (0,)), ((), ())), preferred_element_type=jnp.float32
        )
        for s in range(1, sides):
            other = lax.ppermute(
                part, "head", [((d + s) % sides, d) for d in range(sides)]
            )
            total = total + lax.dot_general(
                other, w_rows[s], (((0,), (0,)), ((), ())), preferred_element_type=jnp.float32
            )
        outputs.append(total.astype(jnp.bfloat16))
    return jnp.concatenate(outputs, 0)


def solution(mesh):
    in_specs = (P("tm", None), P(None, "head"), P(None, "head"), P(None, "head"), P())
    out_specs = P("tm", "head")
    return jax.shard_map(body, mesh=mesh, in_specs=in_specs, out_specs=out_specs, check_vma=False)
```

```python
import math

import jax
import jax.numpy as jnp
from jax import lax
from jax.experimental import pallas as pl
from jax.experimental.pallas import tpu as pltpu
from jax.sharding import PartitionSpec as P

DH = 64
PAIR = 2 * DH
WIN = 512
PK = 256
LONG = 1024
BK = 512
NEG = -1e30


def step(q, k, v, state, mask=None):
    s = lax.dot_general(q, k, (((1,), (1,)), ((), ())), preferred_element_type=jnp.float32)
    if mask is not None:
        s = jnp.where(mask, s, NEG)
    new = jnp.max(s, axis=1, keepdims=True)
    if state is not None:
        new = jnp.maximum(state[0], new)
    p = jnp.exp2(s - new).astype(jnp.bfloat16)
    acc = jnp.dot(p, v, preferred_element_type=jnp.float32)
    if state is not None:
        acc = acc + state[1] * jnp.exp2(state[0] - new)
    return new, acc


def lane():
    return lax.broadcasted_iota(jnp.int32, (1, PAIR), 1)


def by_head(x, fill):
    first = lane() < DH
    fill = jnp.broadcast_to(fill, x.shape)
    return jnp.where(first, x, fill), jnp.where(first, fill, x)


def local_kernel(q_ref, k_ref, v_ref, out_ref):
    index = pl.program_id(1)
    bq = q_ref.shape[0]
    qs = by_head(q_ref[...], jnp.zeros((1, PAIR), jnp.bfloat16))
    one = jnp.ones((1, PAIR), jnp.bfloat16)
    base = index * bq
    states = [None, None]
    for t in range(bq // BK):
        rows = pl.ds(pl.multiple_of(base + t * BK, BK), BK)
        k = k_ref[rows, :]
        vs = by_head(v_ref[rows, :], one)
        skip = t * BK
        shape = (bq - skip, BK)
        mask = lax.broadcasted_iota(jnp.int32, shape, 1) <= lax.broadcasted_iota(
            jnp.int32, shape, 0
        )
        for h in range(2):
            if t == 0:
                states[h] = step(qs[h], k, vs[h], None, mask)
            else:
                top, acc = states[h]
                low = step(qs[h][skip:], k, vs[h], (top[skip:], acc[skip:]), mask)
                states[h] = (
                    jnp.concatenate([top[:skip], low[0]], 0),
                    jnp.concatenate([acc[:skip], low[1]], 0),
                )

    def earlier(j, states):
        rows = pl.ds(pl.multiple_of(j * BK, BK), BK)
        k = k_ref[rows, :]
        vs = by_head(v_ref[rows, :], one)
        return tuple(step(qs[h], k, vs[h], states[h]) for h in range(2))

    states = lax.fori_loop(0, index * (bq // BK), earlier, tuple(states))
    out_ref[0] = jnp.where(lane() < DH + DH // 2, states[0][1], states[0][0])
    out_ref[1] = jnp.where(lane() >= DH // 2, states[1][1], states[1][0])


def remote_kernel(q_ref, state_ref, k_ref, v_ref, ones_ref, out_ref):
    qs = by_head(q_ref[...], jnp.zeros((1, PAIR), jnp.bfloat16))
    total = k_ref.shape[0]
    one, two = state_ref[0], state_ref[1]
    states = [
        (one[:, PAIR - 1 :], jnp.where(lane() < DH + DH // 2, one, one[:, DH : DH + 1])),
        (two[:, :1], jnp.where(lane() >= DH // 2, two, two[:, DH - 1 : DH])),
    ]
    for start in range(0, total, BK):
        stop = min(total, start + BK)
        k = k_ref[start:stop]
        vs = by_head(v_ref[start:stop], ones_ref[start:stop])
        for h in range(2):
            states[h] = step(qs[h], k, vs[h], states[h])
    first = lane() < DH
    one, two = states[0][1], states[1][1]
    sums = jnp.where(first, pltpu.roll(one, DH, 1), pltpu.roll(two, DH, 1))
    out_ref[...] = (jnp.where(first, one, two) / sums).astype(jnp.bfloat16)


def local_attention(q, kv):
    block, width = q.shape
    pairs = width // PAIR
    bq = min(LONG, block)
    return pl.pallas_call(
        local_kernel,
        grid=(pairs, block // bq),
        in_specs=[
            pl.BlockSpec((bq, PAIR), lambda p, i: (i, p)),
            pl.BlockSpec((block, PAIR), lambda p, i: (0, p)),
            pl.BlockSpec((block, PAIR), lambda p, i: (0, pairs + p)),
        ],
        out_specs=pl.BlockSpec((2, bq, PAIR), lambda p, i: (p, i, 0)),
        out_shape=jax.ShapeDtypeStruct((2 * pairs, block, PAIR), jnp.float32),
        compiler_params=pltpu.CompilerParams(vmem_limit_bytes=48 * 2**20),
        cost_estimate=pl.CostEstimate(
            flops=8 * width * block * block, bytes_accessed=8 * width * block, transcendentals=0
        ),
    )(q, kv, kv)


def remote_attention(first, rows, q, state, far, ones):
    width = q.shape[1]
    pairs = width // PAIR
    total = far.shape[0]
    chunk = first // rows
    return pl.pallas_call(
        remote_kernel,
        grid=(pairs,),
        in_specs=[
            pl.BlockSpec((rows, PAIR), lambda p: (chunk, p)),
            pl.BlockSpec((2, rows, PAIR), lambda p: (p, chunk, 0)),
            pl.BlockSpec((total, PAIR), lambda p: (0, p)),
            pl.BlockSpec((total, PAIR), lambda p: (0, pairs + p)),
            pl.BlockSpec((total, PAIR), lambda p: (0, 0)),
        ],
        out_specs=pl.BlockSpec((rows, PAIR), lambda p: (0, p)),
        out_shape=jax.ShapeDtypeStruct((rows, width), jnp.bfloat16),
        compiler_params=pltpu.CompilerParams(vmem_limit_bytes=48 * 2**20),
        cost_estimate=pl.CostEstimate(
            flops=width * rows * total, bytes_accessed=width * rows, transcendentals=0
        ),
    )(q, state, far, far, ones)


def from_behind(value, steps):
    count = lax.axis_size("tm")
    return lax.ppermute(value, "tm", [(s, s + steps) for s in range(count - steps)])


def body(frames, w_query, w_key, w_value, w_out):
    block = frames.shape[0]
    width = w_query.shape[1]
    blocks = lax.axis_size("tm")
    sides = lax.axis_size("head")
    depth = 0
    while 2**depth < blocks:
        depth = depth + 1
    here = lax.axis_index("tm")
    side = lax.axis_index("head")
    kv = jnp.dot(
        frames, jnp.concatenate([w_key, w_value], 1), preferred_element_type=jnp.float32
    ).astype(jnp.bfloat16)
    span = block // PK
    pool = jnp.where(
        jnp.arange(PK)[:, None] == jnp.arange(block)[None, :] // span, 1.0 / span, 0.0
    ).astype(jnp.bfloat16)
    pooled = jnp.dot(pool, kv, preferred_element_type=jnp.float32).astype(jnp.bfloat16)
    near = jnp.concatenate([kv[block - WIN :], pooled], 0)
    kv, frames, pooled, near = lax.optimization_barrier((kv, frames, pooled, near))
    got = [from_behind(near, 1)]
    valid = [jnp.full((WIN + PK,), here >= 1)]
    for level in range(1, depth):
        got.append(from_behind(pooled, 2**level))
        valid.append(jnp.full((PK,), here >= 2**level))
    valid = jnp.concatenate(valid, 0)
    factor = DH**-0.5 * math.log2(math.e)
    q = (jnp.dot(frames, w_query, preferred_element_type=jnp.float32) * factor).astype(
        jnp.bfloat16
    )
    state = local_attention(q, kv)
    absent = jnp.where(jnp.arange(2 * width) < width, kv[0], jnp.bfloat16(0))
    far = jnp.where(valid[:, None], jnp.concatenate(got, 0), absent[None, :])
    ones = jnp.broadcast_to(valid[:, None], (valid.shape[0], PAIR)).astype(jnp.bfloat16)

    mine = lax.dynamic_slice_in_dim(w_out, side * width, width, 1)
    w_rows = [
        lax.dynamic_slice_in_dim(mine, ((side + s) % sides) * width, width, 0)
        for s in range(sides)
    ]
    rows = min(512, block)
    outputs = []
    for first in range(0, block, rows):
        part = remote_attention(first, rows, q, state, far, ones)
        total = jnp.dot(part, w_rows[0], preferred_element_type=jnp.float32)
        for s in range(1, sides):
            other = lax.ppermute(part, "head", [((d + s) % sides, d) for d in range(sides)])
            total = total + jnp.dot(other, w_rows[s], preferred_element_type=jnp.float32)
        outputs.append(total.astype(jnp.bfloat16))
    return jnp.concatenate(outputs, 0)


def solution(mesh):
    in_specs = (P("tm", None), P(None, "head"), P(None, "head"), P(None, "head"), P())
    out_specs = P("tm", "head")
    return jax.shard_map(body, mesh=mesh, in_specs=in_specs, out_specs=out_specs, check_vma=False)
```

```python
import math

import jax
import jax.numpy as jnp
from jax import lax
from jax.experimental import pallas as pl
from jax.experimental.pallas import tpu as pltpu
from jax.sharding import PartitionSpec as P

DH = 64
PAIR = 2 * DH
WIN = 512
PK = 256
LONG = 1024
BK = 512
NEG = -1e30


def wide(x, columns):
    return jnp.concatenate([x] * (columns // PAIR), 1)


def step(q, k, v, state, mask=None):
    s = lax.dot_general(q, k, (((1,), (1,)), ((), ())), preferred_element_type=jnp.float32)
    if mask is not None:
        s = jnp.where(mask, s, NEG)
    new = jnp.broadcast_to(jnp.max(s, axis=1, keepdims=True), (s.shape[0], PAIR))
    if state is not None:
        new = jnp.maximum(state[0], new)
    p = jnp.exp2(s - wide(new, s.shape[1])).astype(jnp.bfloat16)
    acc = jnp.dot(p, v, preferred_element_type=jnp.float32)
    if state is not None:
        acc = acc + state[1] * jnp.exp2(state[0] - new)
    return new, acc


def lane():
    return lax.broadcasted_iota(jnp.int32, (1, PAIR), 1)


def by_head(x, fill):
    first = lane() < DH
    fill = jnp.broadcast_to(fill, x.shape)
    return jnp.where(first, x, fill), jnp.where(first, fill, x)


def local_kernel(q_ref, k_ref, v_ref, acc_ref, top_ref):
    index = pl.program_id(1)
    bq = q_ref.shape[0]
    qs = by_head(q_ref[...], jnp.zeros((1, PAIR), jnp.bfloat16))
    one = jnp.ones((1, PAIR), jnp.bfloat16)
    base = index * bq
    for t in range(bq // BK):
        rows = pl.ds(pl.multiple_of(base + t * BK, BK), BK)
        k = k_ref[rows, :]
        vs = by_head(v_ref[rows, :], one)
        skip = t * BK
        shape = (bq - skip, BK)
        mask = lax.broadcasted_iota(jnp.int32, shape, 1) <= lax.broadcasted_iota(
            jnp.int32, shape, 0
        )
        for h in range(2):
            state = None if t == 0 else (top_ref[h, skip:], acc_ref[h, skip:])
            top_ref[h, skip:], acc_ref[h, skip:] = step(qs[h][skip:], k, vs[h], state, mask)

    def earlier(j, carry):
        states = [(top_ref[h], acc_ref[h]) for h in range(2)]
        for t in range(bq // BK):
            rows = pl.ds(pl.multiple_of(j * bq + t * BK, BK), BK)
            k = k_ref[rows, :]
            vs = by_head(v_ref[rows, :], one)
            for h in range(2):
                states[h] = step(qs[h], k, vs[h], states[h])
        for h in range(2):
            top_ref[h], acc_ref[h] = states[h]
        return carry

    lax.fori_loop(0, index, earlier, 0)


def remote_kernel(q_ref, acc_ref, top_ref, zero_ref, ones_ref, *refs):
    *far, out_ref = refs
    qs = by_head(q_ref[...], jnp.zeros((1, PAIR), jnp.bfloat16))
    pieces = [
        (k_ref, v_ref, start)
        for k_ref, v_ref in zip(far[::2], far[1::2])
        for start in range(0, k_ref.shape[0], PK)
    ]
    states = [None, None]
    group = BK // PK
    for first in range(0, len(pieces), group):
        tile = pieces[first : first + group]
        k = jnp.concatenate([k_ref[at : at + PK] for k_ref, _, at in tile], 0)
        v = jnp.concatenate([v_ref[at : at + PK] for _, v_ref, at in tile], 0)
        ones = ones_ref[first * PK : (first + len(tile)) * PK]
        k = k + (1 - ones) * zero_ref[:1]
        vs = by_head(v, ones)
        for h in range(2):
            states[h] = step(qs[h], k, vs[h], states[h])
    merged = []
    for h in range(2):
        top, acc = states[h]
        new = jnp.maximum(top, top_ref[h])
        merged.append(acc * jnp.exp2(top - new) + acc_ref[h] * jnp.exp2(top_ref[h] - new))
    first = lane() < DH
    one, two = merged
    sums = jnp.where(first, pltpu.roll(one, DH, 1), pltpu.roll(two, DH, 1))
    out_ref[...] = (jnp.where(first, one, two) / sums).astype(jnp.bfloat16)


def local_attention(first, count, q, kv):
    block, width = q.shape
    pairs = width // PAIR
    bq = min(LONG, block)
    return pl.pallas_call(
        local_kernel,
        grid=(count, block // bq),
        in_specs=[
            pl.BlockSpec((bq, PAIR), lambda p, i: (i, first + p)),
            pl.BlockSpec((block, PAIR), lambda p, i: (0, first + p)),
            pl.BlockSpec((block, PAIR), lambda p, i: (0, pairs + first + p)),
        ],
        out_specs=[pl.BlockSpec((2, bq, PAIR), lambda p, i: (p, i, 0))] * 2,
        out_shape=[jax.ShapeDtypeStruct((2 * count, block, PAIR), jnp.float32)] * 2,
        compiler_params=pltpu.CompilerParams(vmem_limit_bytes=48 * 2**20),
        cost_estimate=pl.CostEstimate(
            flops=8 * count * PAIR * block * block,
            bytes_accessed=8 * width * block,
            transcendentals=0,
        ),
    )(q, kv, kv)


def remote_attention(first, count, chunk, rows, q, state, kv, ones, far):
    pairs = q.shape[1] // PAIR
    total = ones.shape[0]
    far_specs, far_args = [], []
    for piece in far:
        far_specs.append(pl.BlockSpec((piece.shape[0], PAIR), lambda p: (0, first + p)))
        far_specs.append(pl.BlockSpec((piece.shape[0], PAIR), lambda p: (0, pairs + first + p)))
        far_args += [piece, piece]
    return pl.pallas_call(
        remote_kernel,
        grid=(count,),
        in_specs=[
            pl.BlockSpec((rows, PAIR), lambda p: (chunk, first + p)),
            pl.BlockSpec((2, rows, PAIR), lambda p: (p, chunk, 0)),
            pl.BlockSpec((2, rows, PAIR), lambda p: (p, chunk, 0)),
            pl.BlockSpec((16, PAIR), lambda p: (0, first + p)),
            pl.BlockSpec((total, PAIR), lambda p: (0, 0)),
            *far_specs,
        ],
        out_specs=pl.BlockSpec((rows, PAIR), lambda p: (0, p)),
        out_shape=jax.ShapeDtypeStruct((rows, count * PAIR), jnp.bfloat16),
        compiler_params=pltpu.CompilerParams(vmem_limit_bytes=48 * 2**20),
        cost_estimate=pl.CostEstimate(
            flops=PAIR * count * rows * total,
            bytes_accessed=PAIR * count * rows,
            transcendentals=0,
        ),
    )(q, *state, kv, ones, *far_args)


def send(value, sources, steps):
    return lax.ppermute(value, "tm", [(s, s + steps) for s in sources])


def body(frames, w_query, w_key, w_value, w_out):
    block = frames.shape[0]
    width = w_query.shape[1]
    blocks = lax.axis_size("tm")
    sides = lax.axis_size("head")
    depth = 0
    while 2**depth < blocks:
        depth = depth + 1
    here = lax.axis_index("tm")
    side = lax.axis_index("head")
    kv = jnp.dot(
        frames, jnp.concatenate([w_key, w_value], 1), preferred_element_type=jnp.float32
    ).astype(jnp.bfloat16)
    span = block // PK
    pool = jnp.where(
        jnp.arange(PK)[:, None] == jnp.arange(block)[None, :] // span, 1.0 / span, 0.0
    ).astype(jnp.bfloat16)
    pooled = jnp.dot(pool, kv, preferred_element_type=jnp.float32).astype(jnp.bfloat16)
    near = jnp.concatenate([kv[block - WIN :], pooled], 0)
    kv, frames, pooled, near = lax.optimization_barrier((kv, frames, pooled, near))
    relay = 4 if blocks > 4 else 0
    early = {0: send(near, range(blocks - 1), 1)}
    for level in range(1, depth):
        if 2**level > 2 * relay or 2**level == relay or not relay:
            early[level] = send(pooled, range(blocks - 2**level), 2**level)
    if relay:
        direct = [s for s in range(blocks - 2) if s % 4 < 2 or s + 4 >= blocks]
        early[1] = send(pooled, direct, 2)
    valid = [jnp.full((WIN + PK,), here >= 1)]
    for level in range(1, depth):
        valid.append(jnp.full((PK,), here >= 2**level))
    valid = jnp.concatenate(valid, 0)
    ones = jnp.broadcast_to(valid[:, None], (valid.shape[0], PAIR)).astype(jnp.bfloat16)
    factor = DH**-0.5 * math.log2(math.e)
    q = (jnp.dot(frames, w_query, preferred_element_type=jnp.float32) * factor).astype(
        jnp.bfloat16
    )
    pairs = width // PAIR
    count = max(1, pairs // 2)
    groups = range(0, pairs, count)
    states = []
    for first in groups:
        states.append(local_attention(first, count, q, kv))
        if first == 0 and relay:
            early[2], states[0], q, kv = lax.optimization_barrier((early[2], states[0], q, kv))
            indirect = [s for s in range(blocks - 2) if s not in direct]
            back = lax.ppermute(early[2], "tm", [(s + 4, s + 2) for s in indirect])
            if depth > 3:
                early[3] = lax.ppermute(
                    early[2], "tm", [(s + 4, s + 8) for s in range(blocks - 8)]
                )
            early[1] = early[1] + back
    far = [early[level] for level in range(depth)]

    mine = lax.dynamic_slice_in_dim(w_out, side * width, width, 1)
    rows = min(LONG, block)
    outputs = []
    for chunk in range(block // rows):
        total = None
        for first, state in zip(groups, states):
            part = remote_attention(first, count, chunk, rows, q, state, kv, ones, far)
            for s in range(sides):
                piece = part
                if s:
                    piece = lax.ppermute(
                        part, "head", [((d + s) % sides, d) for d in range(sides)]
                    )
                start = ((side + s) % sides) * width + first * PAIR
                w_rows = lax.dynamic_slice_in_dim(mine, start, count * PAIR, 0)
                term = jnp.dot(piece, w_rows, preferred_element_type=jnp.float32)
                total = term if total is None else total + term
        outputs.append(total.astype(jnp.bfloat16))
    return jnp.concatenate(outputs, 0)


def solution(mesh):
    in_specs = (P("tm", None), P(None, "head"), P(None, "head"), P(None, "head"), P())
    out_specs = P("tm", "head")
    return jax.shard_map(body, mesh=mesh, in_specs=in_specs, out_specs=out_specs, check_vma=False)
```
